32 devices in a mesh: groups: 2 (over y), atoms: 16 (over z, x, core).
Axes of the slice: x: 2, y: 2, z: 4, core: 2. Of those that a mesh axis runs over, the one named last changes fastest.
Arguments:
- particle_coordinates: float32 [3, 4096], P(None, ('groups', 'atoms')), parts along dimension 1, may hold values from 0 to 72
- integer_lattice_modes: int32 [3, 4096], replicated, may hold values from -6 to 6
- hidden_embeddings: bfloat16 [2, 4096, 128], P(None, ('groups', 'atoms')), parts along dimension 1, may hold values from -6 to 6
- cached_density_modes: bfloat16 [4, 4096, 256], P('groups'), parts along dimension 0, may hold values from -6 to 6
- spectral_kernels: bfloat16 [2, 4096, 128], replicated, may hold values from -4 to 4
- final_embedding_adjoint: bfloat16 [4096, 128], P(('groups', 'atoms')), parts along dimension 0, may hold values from -6 to 6
- particle_result_line: int32 [4096], P(('groups', 'atoms')), parts along dimension 0, may hold values from 0 to 2047, as said below
Outputs:
- feat_grad: float32 [4096, 128], P(('groups', 'atoms')), parts along dimension 0
- pos_grad: float32 [3, 4096], P(None, ('groups', 'atoms')), parts along dimension 1
- filter_grad: float32 [2, 8192, 128], P(None, ('groups', 'atoms')), parts along dimension 1
The draws below stay inside these ranges and needn't reach their ends.
There are 2 independent parts, one for each index of `groups`. The reference program is written for one: setup_inputs(seed, part) draws one part's arguments, and reference() takes and returns one part's arrays. A program takes and returns all parts, laid end to end along the dimension named above; an argument that names none is the same for every part. Nothing has to cross between parts.
Inputs may be any that keep to these rules, and one draw needn't show every extreme that they name: `particle_result_line`: a permutation of the atoms; the atoms of each aligned block of 128 rows send exactly the same number of atoms to every aligned block of 128 output rows.
All inputs are finite; a program needn't handle non-finite values.
Results may differ from the reference program's by a relative error of at most 0.0075.
Values may be sent and summed in bfloat16 or wider, within the bound.
No kernel may reach another device: no remote copies, remote signals or barrier semaphores. Data moves between devices by JAX's collectives and lax.ppermute only.
A program may use at most 128 MiB of HBM per device.

```python
import math
import jax
import jax.numpy as jnp
from jax import lax

CH = 128
LATTICE_WAVES = 4096
BLOCKS = 2
BOX = 72
A_DEV = 128
ATOMS = 2048


def permute_one(key_item, base_list):
    return jax.random.permutation(key_item, base_list)


def draw_particle_result_line(key, part):
    blocks = ATOMS // A_DEV
    per_block = A_DEV // blocks
    base_list = jnp.repeat(jnp.arange(blocks, dtype=jnp.int32), per_block)
    key_list = jax.random.split(jax.random.fold_in(key, 11), blocks)
    target = jax.vmap(permute_one, in_axes=(0, None))(key_list, base_list).reshape(-1)
    onehot = (target[:, None] == jnp.arange(blocks, dtype=jnp.int32)[None, :]).astype(jnp.int32)
    ranking = jnp.sum(jnp.cumsum(onehot, axis=0) * onehot, axis=1) - 1
    slot_keys = jax.random.split(jax.random.fold_in(key, 23), blocks)
    tables = jax.vmap(permute_one, in_axes=(0, None))(slot_keys, jnp.arange(A_DEV, dtype=jnp.int32))
    slot_pos = tables[target, ranking]
    return (target * A_DEV + slot_pos).astype(jnp.int32)


def plant(entries, rng, smallest, largest):
    spot = [jax.random.randint(jax.random.fold_in(rng, axis), (), 0, length) for axis, length in enumerate(entries.shape)]
    widest = entries.shape.index(max(entries.shape))
    next_to = spot[:widest] + [(spot[widest] + 1) % entries.shape[widest]] + spot[widest + 1:]
    return entries.at[tuple(spot)].set(smallest).at[tuple(next_to)].set(largest)


def level_of(rng, shape, cuts, least, high):
    factor_of = 1.0
    for axis_at, blocks in cuts:
        draws = jax.random.uniform(jax.random.fold_in(jax.random.fold_in(rng, 6), axis_at), (blocks,), jnp.float32, least / len(cuts), high / len(cuts))
        factor_of = factor_of * jnp.repeat(jnp.exp(draws), shape[axis_at] // blocks).reshape((-1,) + (1,) * (len(shape) - 1 - axis_at))
    return factor_of


def bell_draw(rng, dims, deviation, most, shards=(), kind=jnp.bfloat16):
    loudness = level_of(rng, dims, shards, -0.22, 0.18) if shards else 1.0
    array = jax.random.normal(rng, dims, jnp.float32) * deviation * loudness
    return jnp.minimum(jnp.maximum(array, -most), most).astype(kind)


def setup_inputs(seed: int = 0, part: int = 0) -> dict:
    arg_keys = jax.random.split(jax.random.key(seed), 8)
    own_keys = jax.random.split(jax.random.fold_in(arg_keys[7], part), 8)
    return {
        "particle_coordinates": jnp.clip(72.0 * jax.random.uniform(own_keys[0], (3, ATOMS), jnp.float32) ** level_of(own_keys[0], (3, ATOMS), ((1, 16),), -0.2, 0.2), 0.0, 72.0),
        "integer_lattice_modes": plant(jax.random.randint(arg_keys[1], (3, LATTICE_WAVES), -6, 7), jax.random.fold_in(arg_keys[1], 1), -6, 6).astype(jnp.int32),
        "hidden_embeddings": bell_draw(own_keys[2], (BLOCKS, ATOMS, CH), 1.0, 6.0, ((1, 16),)),
        "cached_density_modes": bell_draw(own_keys[3], (BLOCKS, LATTICE_WAVES, 2 * CH), 1.0, 6.0),
        "spectral_kernels": bell_draw(arg_keys[4], (BLOCKS, LATTICE_WAVES, CH), 1.0, 4.0),
        "final_embedding_adjoint": bell_draw(own_keys[5], (ATOMS, CH), 1.0, 6.0, ((0, 16),)),
        "particle_result_line": draw_particle_result_line(jax.random.fold_in(jax.random.fold_in(arg_keys[7], part), 71), part),
    }


def angle_terms(particle_locations, integer_lattice_modes):
    lattice_mode = integer_lattice_modes.astype(jnp.float32)
    angles = (particle_locations[0][:, None] * lattice_mode[0][None, :] + particle_locations[1][:, None] * lattice_mode[1][None, :] + particle_locations[2][:, None] * lattice_mode[2][None, :]) * (2.0 * math.pi / BOX)
    return jnp.cos(angles).astype(jnp.bfloat16), jnp.sin(angles).astype(jnp.bfloat16)


def silu_slope(values_in):
    logistic = jax.nn.sigmoid(values_in)
    return logistic * (1.0 + values_in * (1.0 - logistic))


def reference(particle_coordinates, integer_lattice_modes, hidden_embeddings, cached_density_modes, spectral_kernels, final_embedding_adjoint, particle_result_line):
    row_block = min(1024, ATOMS)
    row_count = ATOMS // row_block
    k_scale = LATTICE_WAVES ** -0.5
    a_scale = ATOMS ** -0.5
    two_pi_box = 2.0 * math.pi / BOX
    lattice_mode = integer_lattice_modes.astype(jnp.float32)
    coord_blocks = particle_coordinates.reshape(3, row_count, row_block).transpose(1, 0, 2)
    cotangent = final_embedding_adjoint.astype(jnp.float32)
    pos_total = jnp.zeros((3, ATOMS), jnp.float32)
    filter_parts = []
    for layer_index in range(BLOCKS - 1, -1, -1):
        feature = hidden_embeddings[layer_index]
        saved_block = cached_density_modes[layer_index].astype(jnp.float32)
        doubled = jnp.concatenate([spectral_kernels[layer_index], spectral_kernels[layer_index]], axis=1).astype(jnp.float32)
        filtered = (saved_block * doubled).astype(jnp.bfloat16)
        cot_blocks = cotangent.reshape(row_count, row_block, CH)

        def first_pass(adjoint, inputs):
            particle_locations, cot_rows = inputs
            even_trig_term, odd_trig_term = angle_terms(particle_locations, integer_lattice_modes)
            message = k_scale * (jnp.dot(even_trig_term, filtered[:, :CH], preferred_element_type=jnp.float32) + jnp.dot(odd_trig_term, filtered[:, CH:], preferred_element_type=jnp.float32))
            msg_grad = (cot_rows * silu_slope(message)).astype(jnp.bfloat16)
            adjoint = adjoint + jnp.concatenate([jnp.dot(even_trig_term.T, msg_grad, preferred_element_type=jnp.float32), jnp.dot(odd_trig_term.T, msg_grad, preferred_element_type=jnp.float32)], axis=1)
            return adjoint, msg_grad

        adjoint, msg_blocks = lax.scan(first_pass, jnp.zeros((LATTICE_WAVES, 2 * CH), jnp.float32), (coord_blocks, cot_blocks))
        adjoint = k_scale * adjoint
        filter_parts.append(adjoint[:, :CH] * saved_block[:, :CH] + adjoint[:, CH:] * saved_block[:, CH:])
        factor_grad = (adjoint * doubled).astype(jnp.bfloat16)
        feat_blocks = feature.reshape(row_count, row_block, CH)

        def second_pass(inputs):
            particle_locations, msg_grad, feat_rows = inputs
            even_trig_term, odd_trig_term = angle_terms(particle_locations, integer_lattice_modes)
            feat_add = a_scale * (jnp.dot(even_trig_term, factor_grad[:, :CH], preferred_element_type=jnp.float32) + jnp.dot(odd_trig_term, factor_grad[:, CH:], preferred_element_type=jnp.float32))
            cos_weight = k_scale * jnp.dot(msg_grad, filtered[:, :CH].T, preferred_element_type=jnp.float32) + a_scale * jnp.dot(feat_rows, factor_grad[:, :CH].T, preferred_element_type=jnp.float32)
            sin_weight = k_scale * jnp.dot(msg_grad, filtered[:, CH:].T, preferred_element_type=jnp.float32) + a_scale * jnp.dot(feat_rows, factor_grad[:, CH:].T, preferred_element_type=jnp.float32)
            dtheta = even_trig_term.astype(jnp.float32) * sin_weight - odd_trig_term.astype(jnp.float32) * cos_weight
            pos_add = two_pi_box * jnp.dot(lattice_mode, dtheta.T, precision=lax.Precision.HIGHEST)
            return feat_add, pos_add

        feat_add, pos_add = lax.map(second_pass, (coord_blocks, msg_blocks, feat_blocks))
        cotangent = cotangent + feat_add.reshape(ATOMS, CH)
        pos_total = pos_total + pos_add.transpose(1, 0, 2).reshape(3, ATOMS)
    filter_grad = jnp.stack(filter_parts[::-1])
    feat_grad = jnp.zeros((ATOMS, CH), jnp.float32).at[particle_result_line].set(cotangent)
    pos_grad = jnp.zeros((3, ATOMS), jnp.float32).at[:, particle_result_line].set(pos_total)
    return feat_grad, pos_grad, filter_grad
```

```python
import functools
import math

import jax
import jax.numpy as jnp
from jax import lax
from jax.experimental import pallas as pl
from jax.experimental.pallas import tpu as pltpu
from jax.sharding import PartitionSpec as P

BOX = 72
F32 = jnp.float32
BF16 = jnp.bfloat16


SIN_TURN = (
    6.283182818519537, -41.341421395846474, 81.59618380218637, -76.58009981278215,
    41.205391752072295, -12.271257446632072,
)
COS_TURN = (
    0.9999992216454128, -19.73898252044836, 64.92872667203969, -85.27239717269248,
    58.794038140320986, -21.07677956285326,
)
ROUNDER = 12582912.0

NN = (((1,), (0,)), ((), ()))
NT = (((1,), (1,)), ((), ()))
TN = (((0,), (0,)), ((), ()))
EXTRA = 16


def mm(a, b, dims=NN):
    return lax.dot_general(a, b, dims, preferred_element_type=F32)


def horner(coefs, u):
    acc = coefs[-1] * u + coefs[-2]
    for c in coefs[-3::-1]:
        acc = acc * u + c
    return acc


def cos_sin_turns(t):
    r = t - ((t + ROUNDER) - ROUNDER)
    u = r * r
    return horner(COS_TURN, u).astype(BF16), (r * horner(SIN_TURN, u)).astype(BF16)


def silu_slope(x):
    s = 1.0 / (1.0 + jnp.exp(-x))
    return s * (1.0 + x * (1.0 - s))


def in_pieces(x):
    hi = x.astype(BF16).astype(F32)
    mid = (x - hi).astype(BF16).astype(F32)
    low = (x - hi - mid).astype(BF16).astype(F32)
    return jnp.concatenate([hi, mid, low], axis=0)


def thrice(n):
    zero = jnp.zeros((EXTRA - 9, n.shape[1]), F32)
    return jnp.concatenate([n, n, n, zero], axis=0).astype(BF16)


def atom_kernel(k_scale, coords, line, lattice, modes, kernels, cot, payload, slope0, acc):
    step = pl.program_id(0)
    atoms, ch = cot.shape

    @pl.when(step == 0)
    def _():
        acc[...] = jnp.zeros_like(acc)
        where_to = line[...]
        block = where_to // atoms
        slot = where_to - block * atoms
        payload[atoms:] = jnp.concatenate(
            [
                in_pieces(coords[...] * (1.0 / BOX)),
                block.astype(F32), slot.astype(F32), jnp.zeros((EXTRA - 11, atoms), F32),
            ],
            axis=0,
        ).astype(BF16)

    n = thrice(lattice[...].astype(F32))
    c, s = cos_sin_turns(mm(payload[atoms:], n, TN))
    f1 = kernels[1]
    f0 = kernels[0]
    cos_filt = jnp.concatenate([modes[1, :, :ch] * f1, modes[0, :, :ch] * f0], axis=1)
    sin_filt = jnp.concatenate([modes[1, :, ch:] * f1, modes[0, :, ch:] * f0], axis=1)
    acc[...] += mm(c, cos_filt) + mm(s, sin_filt)

    @pl.when(step == pl.num_programs(0) - 1)
    def _():
        slope = silu_slope(k_scale * acc[...])
        payload[:atoms] = (cot[...].astype(F32) * slope[:, :ch]).astype(BF16)
        slope0[...] = slope[:, ch:]


def own_kernel(idx, lattice, modes, kernels, saved, filt, filters, lattice16):
    own, ch = filters.shape[1:]
    n_modes = lattice.shape[1]
    saved[...] = modes[...]
    filters[...] = kernels[...]
    for b in range(modes.shape[0]):
        f = kernels[b]
        filt[b, :own] = modes[b, :, :ch] * f
        filt[b, own:] = modes[b, :, ch:] * f
    rows = jnp.concatenate([lattice[...].astype(F32), jnp.zeros((5, n_modes), F32)], axis=0)
    rolled = pltpu.roll(rows, n_modes - idx[0] * own, 1)
    lattice16[...] = thrice(rolled[:3, :own])


def stack_kernel(*refs):
    out = refs[-1]
    at = 0
    for ref in refs[:-1]:
        out[at : at + ref.shape[0]] = ref[...]
        at += ref.shape[0]


def trig_kernel(first, second, lattice16, tile):
    half, rows, atoms = first.shape
    modes = lattice16.shape[1]
    n = lattice16[...]
    pair = min(2, half)
    for k, ref in enumerate((first, second)):

        def one(p, _, k=k, ref=ref):
            x = jnp.concatenate(
                [ref[p * pair + j, rows - EXTRA :, :] for j in range(pair)], axis=1
            )
            c, s = cos_sin_turns(mm(n, x, TN))
            at = pl.ds(pl.multiple_of((k * half + p * pair) * atoms, atoms), pair * atoms)
            tile[:modes, at] = c
            tile[modes:, at] = s
            return 0

        lax.fori_loop(0, half // pair, one, 0)


def gather_rows(first, second, start, count):
    ch = first.shape[2]
    return jnp.concatenate(
        [r[:, start : start + count, :].reshape(-1, ch) for r in (first, second)], axis=0
    )


def adjoint_part(b, k_scale, ratio, tile, m, saved, filters):
    own, ch = filters.shape[1:]
    adj = k_scale * mm(tile[...], m)
    modes = saved[b].astype(F32)
    f = filters[b].astype(F32)
    filter_grad = adj[:own] * modes[:, :ch] + adj[own:] * modes[:, ch:]
    f = f * ratio
    factor = jnp.concatenate([adj[:own] * f, adj[own:] * f], axis=0).astype(BF16)
    return filter_grad, factor


def pos_part(b, k_scale, tile, m, h, filt, factor, lattice16):
    own = lattice16.shape[1]
    w = jnp.concatenate([filt[b], factor], axis=1)
    weight = mm(w, jnp.concatenate([m, h], axis=1), NT)
    dtheta = tile[:own].astype(F32) * weight[own:] - tile[own:].astype(F32) * weight[:own]
    return (2.0 * math.pi / BOX * k_scale) * mm(lattice16[:8], dtheta.astype(BF16))


def block1_kernel(k_scale, ratio, tile, first, second, saved, filters, fgrad, factor, send, keep):
    half = first.shape[0]
    atoms = send.shape[2]
    m = gather_rows(first, second, 0, atoms)
    fg, fac = adjoint_part(1, k_scale, ratio, tile, m, saved, filters)
    fgrad[...] = fg
    factor[...] = fac
    add = k_scale * mm(fac.T, tile[...])
    for p in range(half):
        keep[p] = add[:, p * atoms : (p + 1) * atoms]
        send[p] = add[:, (half + p) * atoms : (half + p + 1) * atoms].astype(BF16)


def pos1_kernel(k_scale, tile, first, second, h_first, h_second, filt, factor, lattice16, pos):
    atoms = first.shape[2]
    m = gather_rows(first, second, 0, atoms)
    h = gather_rows(h_first, h_second, atoms, atoms)
    pos[...] = pos_part(1, k_scale, tile, m, h, filt, factor[...], lattice16)


def block0_kernel(
    k_scale, ratio, idx, order, tile, first, second, h_first, h_second, c_first, c_second,
    saved, filters, filt, lattice16, pos1, cot, fgrad, send, keep, x, block, slot,
):
    half, atoms, ch = first.shape
    m = gather_rows(first, second, 0, atoms)
    h = gather_rows(h_first, h_second, 0, atoms)
    fg, fac = adjoint_part(0, k_scale, ratio, tile, m, saved, filters)
    fgrad[...] = fg
    add = k_scale * mm(fac.T, tile[...])
    pos = pos1[...] + pos_part(0, k_scale, tile, m, h, filt, fac, lattice16)
    x[:ch] = add.astype(BF16)
    x[:ch, :atoms] = (add[:, :atoms] + cot[...]).astype(BF16)
    x[ch:] = jnp.concatenate([pos, jnp.zeros_like(pos)], axis=0).astype(BF16)
    for k, ref in enumerate((c_first, c_second)):
        for p in range(half):
            at = pl.ds((k * half + p) * atoms, atoms)
            block[:, at] = ref[p, atoms + 9 : atoms + 10, :].astype(F32)
            slot[:, at] = ref[p, atoms + 10 : atoms + 11, :].astype(F32)
    lanes = lax.broadcasted_iota(jnp.int32, (atoms, block.shape[1]), 0).astype(F32).astype(BF16)
    me = idx[0]

    def placed(q):
        target = (order[q] ^ me).astype(F32)
        here = jnp.where(block[...] == target, slot[...], -1.0).astype(BF16)
        hot = jnp.where(here == lanes, jnp.ones_like(lanes), jnp.zeros_like(lanes))
        return mm(x[...], hot, NT)

    def kept(q, _):
        keep[q] = placed(q)
        return 0

    def sent(q, _):
        send[q] = placed(half + q).astype(BF16)
        return 0

    unroll = half <= 8
    lax.fori_loop(0, half, kept, 0, unroll=unroll)
    lax.fori_loop(0, half, sent, 0, unroll=unroll)


def reduce_kernel(got_n, keep, *refs):
    got = refs[:got_n]
    rest, *sends = refs[got_n:]
    width = rest.shape[0]
    for p in range(keep.shape[0]):
        total = functools.reduce(lambda a, g: a + g[p].astype(F32), got, keep[p])
        if p < width:
            rest[p] = total
        else:
            sends[p // width - 1][p % width] = total.astype(BF16)


def total_of(keep, got):
    return functools.reduce(lambda a, g: a + g[0].astype(F32), got, keep[0])


def finish1_kernel(keep, *refs):
    got = refs[:-4]
    cot, slope0, cot_t, msg = refs[-4:]
    new = cot[...].astype(F32).T + total_of(keep, got)
    cot_t[...] = new
    msg[...] = (new.T * slope0[...]).astype(BF16)


def finish0_kernel(keep, *refs):
    got = refs[:-2]
    feat, pos = refs[-2:]
    total = total_of(keep, got)
    ch = feat.shape[1]
    feat[...] = total[:ch].T
    pos[...] = total[ch : ch + 3]


def filters_kernel(f0, f1, out):
    out[0] = f0[...]
    out[1] = f1[...]


VMEM = pl.BlockSpec(memory_space=pltpu.VMEM)
PARAMS = pltpu.CompilerParams(vmem_limit_bytes=24 << 20)
SMEM = pl.BlockSpec(memory_space=pltpu.SMEM)


def near(x):
    return pltpu.with_memory_space_constraint(x, pltpu.VMEM)


def far(x):
    return pltpu.with_memory_space_constraint(x, pltpu.HBM)


def call(kernel, outs, *args, scalars=0, scratch=()):
    specs = [SMEM] * scalars + [VMEM] * (len(args) - scalars)
    args = args[:scalars] + tuple(near(a) for a in args[scalars:])
    return pl.pallas_call(
        kernel,
        out_shape=outs,
        in_specs=specs,
        out_specs=jax.tree.map(lambda _: VMEM, outs),
        scratch_shapes=list(scratch),
        compiler_params=PARAMS,
    )(*args)


def buf(shape, dtype):
    return pltpu.VMEM(shape, dtype)


def sds(shape, dtype):
    return jax.ShapeDtypeStruct(shape, dtype)


def swap(x, mask, devices):
    return lax.ppermute(x, "atoms", [(i, i ^ mask) for i in range(devices)])


def phase_plan(devices):
    bits = devices.bit_length() - 1
    high = [[1 << b] for b in range(bits - 1, 2, -1)]
    middle = [[2, 4, 6]] if bits >= 3 else [[2]]
    return high + middle + [[1]]


def position_order(plan):
    order = [0]
    for masks in plan:
        order = order + [p ^ m for m in masks for p in order]
    return order


def stack(parts):
    rows = sum(p.shape[0] for p in parts)
    return call(stack_kernel, buf((rows, *parts[0].shape[1:]), parts[0].dtype), *parts)


def gather(x, plan, devices):
    y = x[None]
    for masks in plan[:-1]:
        got = [swap(y, m, devices) for m in masks]
        y = stack([y, *got])
    return y, swap(y, plan[-1][0], devices)


def reduce_blocks(send, keep, plan, devices):
    got = [swap(send, plan[-1][0], devices)]
    for k in range(len(plan) - 2, -1, -1):
        masks = plan[k]
        width = keep.shape[0] // (len(masks) + 1)
        block = (width, *keep.shape[1:])
        keep, *sends = call(
            functools.partial(reduce_kernel, len(got)),
            (buf(block, F32),) + (buf(block, BF16),) * len(masks),
            keep, *got,
        )
        got = [swap(s, m, devices) for s, m in zip(sends, masks)]
    return keep, got


def stages(coords, lattice, hidden, modes, kernels, cot, line):
    blocks = hidden.shape[0]
    channels = hidden.shape[2]
    n_modes = lattice.shape[1]
    atoms = coords.shape[1]
    devices = lax.axis_size("atoms")
    own = n_modes // devices
    half = devices // 2
    total = atoms * devices
    k_scale = n_modes ** (-0.5)
    ratio = total ** (-0.5) / k_scale
    plan = phase_plan(devices)
    order = jnp.asarray(position_order(plan), jnp.int32)
    idx = lax.axis_index("atoms").reshape(1).astype(jnp.int32)

    chunk = min(512, n_modes)
    rows = atoms + EXTRA
    payload, slope0 = pl.pallas_call(
        functools.partial(atom_kernel, k_scale),
        grid=(n_modes // chunk,),
        in_specs=[
            pl.BlockSpec((3, atoms), lambda k: (0, 0)),
            pl.BlockSpec((1, atoms), lambda k: (0, 0)),
            pl.BlockSpec((3, chunk), lambda k: (0, k)),
            pl.BlockSpec((blocks, chunk, 2 * channels), lambda k: (0, k, 0)),
            pl.BlockSpec((blocks, chunk, channels), lambda k: (0, k, 0)),
            pl.BlockSpec((atoms, channels), lambda k: (0, 0)),
        ],
        out_specs=[VMEM, VMEM],
        out_shape=(buf((rows, channels), BF16), buf((atoms, channels), F32)),
        scratch_shapes=[pltpu.VMEM((atoms, 2 * channels), F32)],
        compiler_params=PARAMS,
    )(far(coords), far(line[None]), far(lattice), far(modes), far(kernels), far(cot))

    c_first, c_second = gather(payload, plan, devices)
    own_rows = pl.pallas_call(
        own_kernel,
        grid_spec=pltpu.PrefetchScalarGridSpec(
            num_scalar_prefetch=1,
            grid=(1,),
            in_specs=[
                pl.BlockSpec((3, n_modes), lambda k, i: (0, 0)),
                pl.BlockSpec((blocks, own, 2 * channels), lambda k, i: (0, i[0], 0)),
                pl.BlockSpec((blocks, own, channels), lambda k, i: (0, i[0], 0)),
            ],
            out_specs=[VMEM] * 4,
        ),
        out_shape=(
            buf((blocks, own, 2 * channels), BF16),
            buf((blocks, 2 * own, channels), BF16),
            buf((blocks, own, channels), BF16),
            buf((EXTRA, own), BF16),
        ),
        compiler_params=PARAMS,
    )
    saved, filt, filters, lattice16 = own_rows(idx, far(lattice), far(modes), far(kernels))
    h_first, h_second = gather(hidden.reshape(blocks * atoms, channels), plan, devices)

    tile = call(trig_kernel, buf((2 * own, total), BF16), c_first, c_second, lattice16)
    fgrad1, factor1, send, keep = call(
        functools.partial(block1_kernel, k_scale, ratio),
        (
            buf((own, channels), F32),
            buf((2 * own, channels), BF16),
            buf((half, channels, atoms), BF16),
            buf((half, channels, atoms), F32),
        ),
        tile, c_first, c_second, saved, filters,
    )
    keep, got = reduce_blocks(send, keep, plan, devices)
    cot_t, msg0 = call(
        finish1_kernel,
        (buf((channels, atoms), F32), buf((atoms, channels), BF16)),
        keep, *got, cot, slope0,
    )

    pos1 = call(
        functools.partial(pos1_kernel, k_scale),
        buf((8, total), F32),
        tile, c_first, c_second, h_first, h_second, filt, factor1, lattice16,
    )
    m_first, m_second = gather(msg0, plan, devices)
    fgrad0, send, keep = call(
        functools.partial(block0_kernel, k_scale, ratio),
        (
            buf((own, channels), F32),
            buf((half, rows, atoms), BF16),
            buf((half, rows, atoms), F32),
        ),
        idx, order, tile, m_first, m_second, h_first, h_second, c_first, c_second,
        saved, filters, filt, lattice16, pos1, cot_t,
        scalars=2,
        scratch=(
            pltpu.VMEM((rows, total), BF16),
            pltpu.VMEM((1, total), F32),
            pltpu.VMEM((1, total), F32),
        ),
    )
    filter_grad = pl.pallas_call(
        filters_kernel,
        out_shape=sds((blocks, own, channels), F32),
        in_specs=[VMEM, VMEM],
        compiler_params=PARAMS,
    )(near(fgrad0), near(fgrad1))
    keep, got = reduce_blocks(send, keep, plan, devices)
    feat_grad, pos_grad = pl.pallas_call(
        finish0_kernel,
        out_shape=(sds((atoms, channels), F32), sds((3, atoms), F32)),
        in_specs=[VMEM] * (1 + len(got)),
        compiler_params=PARAMS,
    )(near(keep), *(near(g) for g in got))
    return feat_grad, pos_grad, filter_grad


def solution(mesh):
    in_specs = (
        P(None, ("groups", "atoms")),
        P(),
        P(None, ("groups", "atoms"), None),
        P("groups", None, None),
        P(),
        P(("groups", "atoms"), None),
        P(("groups", "atoms")),
    )
    out_specs = (
        P(("groups", "atoms"), None),
        P(None, ("groups", "atoms")),
        P(None, ("groups", "atoms"), None),
    )
    return jax.shard_map(stages, mesh=mesh, in_specs=in_specs, out_specs=out_specs, check_vma=False)
```

```python
import functools
import math

import jax
import jax.numpy as jnp
from jax import lax
from jax.experimental import pallas as pl
from jax.experimental.pallas import tpu as pltpu
from jax.sharding import PartitionSpec as P

BOX = 72
F32 = jnp.float32
BF16 = jnp.bfloat16


SIN_TURN = (
    6.283182818519537, -41.341421395846474, 81.59618380218637, -76.58009981278215,
    41.205391752072295, -12.271257446632072,
)
COS_TURN = (
    0.9999992216454128, -19.73898252044836, 64.92872667203969, -85.27239717269248,
    58.794038140320986, -21.07677956285326,
)
ROUNDER = 12582912.0

NN = (((1,), (0,)), ((), ()))
NT = (((1,), (1,)), ((), ()))
TN = (((0,), (0,)), ((), ()))
CHUNK = 1024
EXTRA = 16


def mm(a, b, dims=NN):
    return lax.dot_general(a, b, dims, preferred_element_type=F32)


def horner(coefs, u):
    acc = coefs[-1] * u + coefs[-2]
    for c in coefs[-3::-1]:
        acc = acc * u + c
    return acc


def cos_sin_turns(t):
    r = t - ((t + ROUNDER) - ROUNDER)
    u = r * r
    return horner(COS_TURN, u).astype(BF16), (r * horner(SIN_TURN, u)).astype(BF16)


def silu_slope(x):
    s = 1.0 / (1.0 + jnp.exp(-x))
    return s * (1.0 + x * (1.0 - s))


def in_pieces(x):
    hi = x.astype(BF16).astype(F32)
    mid = (x - hi).astype(BF16).astype(F32)
    low = (x - hi - mid).astype(BF16).astype(F32)
    return jnp.concatenate([hi, mid, low], axis=0)


def thrice(n):
    zero = jnp.zeros((EXTRA - 9, n.shape[1]), F32)
    return jnp.concatenate([n, n, n, zero], axis=0).astype(BF16)


def atom_kernel(k_scale, coords, line, lattice, modes, kernels, cot, payload, extra, acc):
    step = pl.program_id(0)
    atoms, ch = cot.shape

    @pl.when(step == 0)
    def _():
        acc[...] = jnp.zeros_like(acc)
        where_to = line[...]
        block = where_to // atoms
        slot = where_to - block * atoms
        payload[atoms:] = jnp.concatenate(
            [
                in_pieces(coords[...] * (1.0 / BOX)),
                block.astype(F32), slot.astype(F32), jnp.zeros((EXTRA - 11, atoms), F32),
            ],
            axis=0,
        ).astype(BF16)
        extra[0] = cot[...]

    n = thrice(lattice[...].astype(F32))
    c, s = cos_sin_turns(mm(payload[atoms:], n, TN))
    f1 = kernels[1]
    f0 = kernels[0]
    cos_filt = jnp.concatenate([modes[1, :, :ch] * f1, modes[0, :, :ch] * f0], axis=1)
    sin_filt = jnp.concatenate([modes[1, :, ch:] * f1, modes[0, :, ch:] * f0], axis=1)
    acc[...] += mm(c, cos_filt) + mm(s, sin_filt)

    @pl.when(step == pl.num_programs(0) - 1)
    def _():
        slope = silu_slope(k_scale * acc[...])
        payload[:atoms] = (cot[...].astype(F32) * slope[:, :ch]).astype(BF16)
        slope0 = slope[:, ch:]
        hi = slope0.astype(BF16)
        extra[1] = hi
        extra[2] = (slope0 - hi.astype(F32)).astype(BF16)


def own_kernel(idx, lattice, modes, kernels, saved, filt, filters, lattice16):
    own, ch = filters.shape[1:]
    n_modes = lattice.shape[1]
    saved[...] = modes[...]
    filters[...] = kernels[...]
    for b in range(modes.shape[0]):
        f = kernels[b]
        filt[b, :own] = modes[b, :, :ch] * f
        filt[b, own:] = modes[b, :, ch:] * f
    rows = jnp.concatenate([lattice[...].astype(F32), jnp.zeros((5, n_modes), F32)], axis=0)
    rolled = pltpu.roll(rows, n_modes - idx[0] * own, 1)
    lattice16[...] = thrice(rolled[:3, :own])


def stack_kernel(*refs):
    out = refs[-1]
    at = 0
    for ref in refs[:-1]:
        out[at : at + ref.shape[0]] = ref[...]
        at += ref.shape[0]


def trig_kernel(first_block, *refs):
    lattice16, tile = refs[0], refs[-1]
    modes = lattice16.shape[1]
    n = lattice16[...]
    for ref in refs[1:-1]:
        count, rows, atoms = ref.shape
        pair = min(2, count)

        def one(p, _, ref=ref, start=first_block, pair=pair, rows=rows, atoms=atoms):
            x = jnp.concatenate(
                [ref[p * pair + j, rows - EXTRA :, :] for j in range(pair)], axis=1
            )
            c, s = cos_sin_turns(mm(n, x, TN))
            at = pl.ds(pl.multiple_of((start + p * pair) * atoms, atoms), pair * atoms)
            tile[:modes, at] = c
            tile[modes:, at] = s
            return 0

        lax.fori_loop(0, count // pair, one, 0)
        first_block += count


def trig_rest_kernel(first_block, tile_in, *refs):
    trig_kernel(first_block, *refs)


def rows_of(refs, start, count):
    ch = refs[0].shape[2]
    return jnp.concatenate(
        [r[:, start : start + count, :].reshape(-1, ch) for r in refs], axis=0
    )


def adjoint_kernel(tile, *refs):
    *blocks, keep, send = refs
    part = mm(tile[...], rows_of(blocks, 0, blocks[0].shape[2]))
    keep[...] = part
    send[...] = part.astype(BF16)


def filtered_adjoint(b, k_scale, ratio, core, keep, got, saved, filters, fgrad):
    own, ch = filters.shape[1:]
    mine = fgrad.shape[0]
    adj = k_scale * (keep[...] + got[...].astype(F32))
    keep[...] = adj
    at = pl.ds(pl.multiple_of(core * mine, mine), mine)
    sin_at = pl.ds(pl.multiple_of(own + core * mine, mine), mine)
    fgrad[...] = keep[at, :] * saved[b, at, :ch].astype(F32) + keep[sin_at, :] * saved[
        b, at, ch:
    ].astype(F32)
    f = filters[b].astype(F32) * ratio
    return jnp.concatenate([adj[:own] * f, adj[own:] * f], axis=0).astype(BF16)


def pos_part(b, k_scale, tile, m, h, filt, factor, lattice16):
    own = lattice16.shape[1]
    w = jnp.concatenate([filt[b], factor], axis=1)
    weight = mm(w, jnp.concatenate([m, h], axis=1), NT)
    dtheta = tile[:own].astype(F32) * weight[own:] - tile[own:].astype(F32) * weight[:own]
    return (2.0 * math.pi / BOX * k_scale) * mm(lattice16[:8], dtheta.astype(BF16))


def block1_kernel(
    k_scale, ratio, core, tile, part, got, saved, filters, fgrad, factor, keep, *refs
):
    *sends, scr = refs
    scr[...] = part[...]
    fac = filtered_adjoint(1, k_scale, ratio, core[0], scr, got, saved, filters, fgrad)
    factor[...] = fac
    add = k_scale * mm(fac.T, tile[...])
    width, _, atoms = keep.shape
    for p in range(add.shape[1] // atoms):
        value = add[:, p * atoms : (p + 1) * atoms]
        if p < width:
            keep[p] = value
        else:
            sends[p // width - 1][p % width] = value.astype(BF16)


def pos1_kernel(k_scale, n, tile, *refs):
    blocks, h_blocks = refs[:n], refs[n : 2 * n]
    filt, factor, lattice16, pos = refs[2 * n :]
    atoms = blocks[0].shape[2]
    m = rows_of(blocks, 0, atoms)
    h = rows_of(h_blocks, atoms, atoms)
    pos[...] = pos_part(1, k_scale, tile, m, h, filt, factor[...], lattice16)


def block0_kernel(k_scale, ratio, n, idx, order, core, tile, part, got, *refs):
    blocks, h_blocks, c_blocks = refs[:n], refs[n : 2 * n], refs[2 * n : 3 * n]
    (
        saved, filters, filt, lattice16, pos1, cot, fgrad, send, keep, x, block, slot, scr,
    ) = refs[3 * n :]
    _, atoms, ch = blocks[0].shape
    half = keep.shape[0]
    m = rows_of(blocks, 0, atoms)
    h = rows_of(h_blocks, 0, atoms)
    scr[...] = part[...]
    fac = filtered_adjoint(0, k_scale, ratio, core[0], scr, got, saved, filters, fgrad)
    add = k_scale * mm(fac.T, tile[...])
    pos = pos1[...] + pos_part(0, k_scale, tile, m, h, filt, fac, lattice16)
    x[:ch] = add.astype(BF16)
    x[:ch, :atoms] = (add[:, :atoms] + cot[...]).astype(BF16)
    x[ch:] = jnp.concatenate([pos, jnp.zeros_like(pos)], axis=0).astype(BF16)
    at = 0
    for ref in c_blocks:
        for p in range(ref.shape[0]):
            block[:, at : at + atoms] = ref[p, atoms + 9 : atoms + 10, :].astype(F32)
            slot[:, at : at + atoms] = ref[p, atoms + 10 : atoms + 11, :].astype(F32)
            at += atoms
    lanes = lax.broadcasted_iota(jnp.int32, (atoms, block.shape[1]), 0).astype(F32).astype(BF16)
    me = idx[0]

    def placed(q):
        target = (order[q] ^ me).astype(F32)
        here = jnp.where(block[...] == target, slot[...], -1.0).astype(BF16)
        hot = jnp.where(here == lanes, jnp.ones_like(lanes), jnp.zeros_like(lanes))
        return mm(x[...], hot, NT)

    def kept(q, _):
        keep[q] = placed(q)
        return 0

    def sent(q, _):
        send[q] = placed(half + q).astype(BF16)
        return 0

    unroll = half <= 8
    lax.fori_loop(0, half, kept, 0, unroll=unroll)
    lax.fori_loop(0, half, sent, 0, unroll=unroll)


def reduce_kernel(got_n, both, keep, *refs):
    got = refs[:got_n]
    rest, *sends = refs[got_n:]
    width = rest.shape[0]
    for p in range(keep.shape[0]):
        total = functools.reduce(lambda a, g: a + g[p].astype(F32), got, keep[p])
        if p < width:
            rest[p] = total
        if both:
            sends[0][p] = total.astype(BF16)
        elif p >= width:
            sends[p // width - 1][p % width] = total.astype(BF16)


def finish1_kernel(keep, got, extra, far_extra, cot_t, msg):
    for j, e in enumerate((extra, far_extra)):
        new = e[0].astype(F32).T + keep[j] + got[1 - j].astype(F32)
        if j == 0:
            cot_t[...] = new
        slope = e[1].astype(F32) + e[2].astype(F32)
        msg[j] = (new.T * slope).astype(BF16)


def finish0_kernel(keep, *refs):
    got = refs[:-2]
    feat, pos = refs[-2:]
    total = functools.reduce(lambda a, g: a + g[0].astype(F32), got, keep[0])
    ch = feat.shape[1]
    feat[...] = total[:ch].T
    pos[...] = total[ch : ch + 3]


def filters_kernel(f0, f1, out):
    out[0] = f0[...]
    out[1] = f1[...]


VMEM = pl.BlockSpec(memory_space=pltpu.VMEM)
PARAMS = pltpu.CompilerParams(vmem_limit_bytes=24 << 20)
SMEM = pl.BlockSpec(memory_space=pltpu.SMEM)


def near(x):
    return pltpu.with_memory_space_constraint(x, pltpu.VMEM)


def far(x):
    return pltpu.with_memory_space_constraint(x, pltpu.HBM)


def call(kernel, outs, *args, scalars=0, scratch=(), alias=None):
    specs = [SMEM] * scalars + [VMEM] * (len(args) - scalars)
    args = args[:scalars] + tuple(near(a) for a in args[scalars:])
    return pl.pallas_call(
        kernel,
        out_shape=outs,
        in_specs=specs,
        out_specs=jax.tree.map(lambda _: VMEM, outs),
        scratch_shapes=list(scratch),
        input_output_aliases=alias or {},
        compiler_params=PARAMS,
    )(*args)


def buf(shape, dtype):
    return pltpu.VMEM(shape, dtype)


def sds(shape, dtype):
    return jax.ShapeDtypeStruct(shape, dtype)


def swap(x, mask, devices):
    return lax.ppermute(x, "atoms", [(i, i ^ mask) for i in range(devices)])


def phase_plan(devices):
    bits = devices.bit_length() - 1
    return [[1 << b] for b in range(bits - 1, 2, -1)] + [[2, 4, 6]]


def position_order(plan):
    order = [0]
    for masks in plan:
        order = order + [p ^ m for m in masks for p in order]
    return order


def stack(parts):
    rows = sum(p.shape[0] for p in parts)
    return call(stack_kernel, buf((rows, *parts[0].shape[1:]), parts[0].dtype), *parts)


def gather(y, plan, devices, start=0):
    for k in range(start, len(plan)):
        got = [swap(y, m, devices) for m in plan[k]]
        if k < len(plan) - 1:
            y = stack([y, *got])
    return [y, *got]


def reduce_blocks(keep, got, plan, devices, both=False):
    for k in range(len(plan) - 1, -1, -1):
        masks = plan[k]
        if got:
            swap_all = both and k == 0
            width = keep.shape[0] if swap_all else keep.shape[0] // (len(masks) + 1)
            block = (width, *keep.shape[1:])
            keep, *sends = call(
                functools.partial(reduce_kernel, len(got), swap_all),
                (buf(block, F32),) + (buf(block, BF16),) * len(masks),
                keep, *got,
            )
        got = [swap(s, m, devices) for s, m in zip(sends, masks)]
    return keep, got


def stages(coords, lattice, hidden, modes, kernels, cot, line):
    blocks = hidden.shape[0]
    channels = hidden.shape[2]
    n_modes = lattice.shape[1]
    atoms = coords.shape[1]
    devices = lax.axis_size("atoms")
    chips = devices // 2
    own = n_modes // chips
    mine = n_modes // devices
    side = atoms * chips
    k_scale = n_modes ** (-0.5)
    ratio = (atoms * devices) ** (-0.5) / k_scale
    plan = phase_plan(devices)
    order = position_order(plan)
    order = jnp.asarray(order + [p ^ 1 for p in order], jnp.int32)
    me = lax.axis_index("atoms").reshape(1).astype(jnp.int32)
    chip = me // 2
    core = me % 2

    chunk = min(CHUNK, n_modes)
    rows = atoms + EXTRA
    payload, extra = pl.pallas_call(
        functools.partial(atom_kernel, k_scale),
        grid=(n_modes // chunk,),
        in_specs=[
            pl.BlockSpec((3, atoms), lambda k: (0, 0)),
            pl.BlockSpec((1, atoms), lambda k: (0, 0)),
            pl.BlockSpec((3, chunk), lambda k: (0, k)),
            pl.BlockSpec((blocks, chunk, 2 * channels), lambda k: (0, k, 0)),
            pl.BlockSpec((blocks, chunk, channels), lambda k: (0, k, 0)),
            pl.BlockSpec((atoms, channels), lambda k: (0, 0)),
        ],
        out_specs=[VMEM, VMEM],
        out_shape=(buf((rows, channels), BF16), buf((3, atoms, channels), BF16)),
        scratch_shapes=[pltpu.VMEM((atoms, 2 * channels), F32)],
        compiler_params=PARAMS,
    )(far(coords), far(line[None]), far(lattice), far(modes), far(kernels), far(cot))

    own_rows = pl.pallas_call(
        own_kernel,
        grid_spec=pltpu.PrefetchScalarGridSpec(
            num_scalar_prefetch=1,
            grid=(1,),
            in_specs=[
                pl.BlockSpec((3, n_modes), lambda k, i: (0, 0)),
                pl.BlockSpec((blocks, own, 2 * channels), lambda k, i: (0, i[0], 0)),
                pl.BlockSpec((blocks, own, channels), lambda k, i: (0, i[0], 0)),
            ],
            out_specs=[VMEM] * 4,
        ),
        out_shape=(
            buf((blocks, own, 2 * channels), BF16),
            buf((blocks, 2 * own, channels), BF16),
            buf((blocks, own, channels), BF16),
            buf((EXTRA, own), BF16),
        ),
        compiler_params=PARAMS,
    )
    saved, filt, filters, lattice16 = own_rows(chip, far(lattice), far(modes), far(kernels))
    c_blocks = gather(payload[None], plan, devices)
    h_blocks = gather(hidden.reshape(1, blocks * atoms, channels), plan, devices)
    n = len(c_blocks)
    far_extra = swap(extra, plan[0][0], devices)

    tile = call(
        functools.partial(trig_kernel, 0), buf((2 * own, side), BF16), lattice16, c_blocks[0]
    )
    tile = call(
        functools.partial(trig_rest_kernel, c_blocks[0].shape[0]),
        buf((2 * own, side), BF16),
        tile, lattice16, *c_blocks[1:],
        alias={0: 0},
    )

    def adjoint(m_blocks):
        part, send = call(
            adjoint_kernel,
            (buf((2 * own, channels), F32), buf((2 * own, channels), BF16)),
            tile, *m_blocks,
        )
        return part, swap(send, 1, devices)

    scr = pltpu.VMEM((2 * own, channels), F32)
    part, got = adjoint(c_blocks)
    width = chips // (len(plan[-1]) + 1)
    fgrad1, factor1, keep, *sends = call(
        functools.partial(block1_kernel, k_scale, ratio),
        (
            buf((mine, channels), F32),
            buf((2 * own, channels), BF16),
            buf((width, channels, atoms), F32),
        )
        + (buf((width, channels, atoms), BF16),) * len(plan[-1]),
        core, tile, part, got, saved, filters,
        scalars=1,
        scratch=(scr,),
    )
    got = [swap(s, m, devices) for s, m in zip(sends, plan[-1])]
    keep, got = reduce_blocks(keep, got, plan[:-1], devices, both=True)
    cot_t, msg0 = call(
        finish1_kernel,
        (buf((channels, atoms), F32), buf((2, atoms, channels), BF16)),
        keep, *got, extra, far_extra,
    )

    pos1 = call(
        functools.partial(pos1_kernel, k_scale, n),
        buf((8, side), F32),
        tile, *c_blocks, *h_blocks, filt, factor1, lattice16,
    )
    m_blocks = gather(msg0, plan, devices, start=1)
    part, got = adjoint(m_blocks)
    fgrad0, send, keep = call(
        functools.partial(block0_kernel, k_scale, ratio, n),
        (
            buf((mine, channels), F32),
            buf((chips, rows, atoms), BF16),
            buf((chips, rows, atoms), F32),
        ),
        me, order, core, tile, part, got, *m_blocks, *h_blocks, *c_blocks,
        saved, filters, filt, lattice16, pos1, cot_t,
        scalars=3,
        scratch=(
            pltpu.VMEM((rows, side), BF16),
            pltpu.VMEM((1, side), F32),
            pltpu.VMEM((1, side), F32),
            scr,
        ),
    )
    got = [swap(send, 1, devices)]
    filter_grad = pl.pallas_call(
        filters_kernel,
        out_shape=sds((blocks, mine, channels), F32),
        in_specs=[VMEM, VMEM],
        compiler_params=PARAMS,
    )(near(fgrad0), near(fgrad1))
    keep, got = reduce_blocks(keep, got, plan, devices)
    feat_grad, pos_grad = pl.pallas_call(
        finish0_kernel,
        out_shape=(sds((atoms, channels), F32), sds((3, atoms), F32)),
        in_specs=[VMEM] * (1 + len(got)),
        compiler_params=PARAMS,
    )(near(keep), *(near(g) for g in got))
    return feat_grad, pos_grad, filter_grad


def solution(mesh):
    in_specs = (
        P(None, ("groups", "atoms")),
        P(),
        P(None, ("groups", "atoms"), None),
        P("groups", None, None),
        P(),
        P(("groups", "atoms"), None),
        P(("groups", "atoms")),
    )
    out_specs = (
        P(("groups", "atoms"), None),
        P(None, ("groups", "atoms")),
        P(None, ("groups", "atoms"), None),
    )
    return jax.shard_map(stages, mesh=mesh, in_specs=in_specs, out_specs=out_specs, check_vma=False)
```

```python
import functools
import math

import jax
import jax.numpy as jnp
from jax import lax
from jax.experimental import pallas as pl
from jax.experimental.pallas import tpu as pltpu
from jax.sharding import PartitionSpec as P

BOX = 72
F32 = jnp.float32
BF16 = jnp.bfloat16


SIN_TURN = (
    6.283182818519537, -41.341421395846474, 81.59618380218637, -76.58009981278215,
    41.205391752072295, -12.271257446632072,
)
COS_TURN = (
    0.9999992216454128, -19.73898252044836, 64.92872667203969, -85.27239717269248,
    58.794038140320986, -21.07677956285326,
)
ROUNDER = 12582912.0

NN = (((1,), (0,)), ((), ()))
NT = (((1,), (1,)), ((), ()))
TN = (((0,), (0,)), ((), ()))
CHUNK = 1024
HOT_LIMIT = 4 << 20
EXTRA = 16


def mm(a, b, dims=NN):
    return lax.dot_general(a, b, dims, preferred_element_type=F32)


def horner(coefs, u):
    acc = coefs[-1] * u + coefs[-2]
    for c in coefs[-3::-1]:
        acc = acc * u + c
    return acc


def cos_sin_turns(t):
    r = t - ((t + ROUNDER) - ROUNDER)
    u = r * r
    return horner(COS_TURN, u).astype(BF16), (r * horner(SIN_TURN, u)).astype(BF16)


def silu_slope(x):
    s = 1.0 / (1.0 + jnp.exp(-x))
    return s * (1.0 + x * (1.0 - s))


def in_pieces(x):
    hi = x.astype(BF16).astype(F32)
    mid = (x - hi).astype(BF16).astype(F32)
    low = (x - hi - mid).astype(BF16).astype(F32)
    return jnp.concatenate([hi, mid, low], axis=0)


def thrice(n):
    zero = jnp.zeros((EXTRA - 9, n.shape[1]), F32)
    return jnp.concatenate([n, n, n, zero], axis=0).astype(BF16)


def atom_kernel(
    k_scale, chunk, coords_far, line_far, lattice_far, modes_far, kernels_far, cot_far,
    payload, slope0, side, coords, line, lattice, modes, kernels, cot, sems,
):
    atoms, ch = cot.shape
    steps = lattice.shape[1] // chunk
    spans = [slice(j * chunk, (j + 1) * chunk) for j in range(steps)]
    small = [
        pltpu.make_async_copy(src, dst, sems.at[k])
        for k, (src, dst) in enumerate(
            ((coords_far, coords), (line_far, line), (lattice_far, lattice), (cot_far, cot))
        )
    ]
    loads = [
        [
            pltpu.make_async_copy(src.at[:, span], dst.at[:, span], sems.at[4 + 2 * j + k])
            for k, (src, dst) in enumerate(((modes_far, modes), (kernels_far, kernels)))
        ]
        for j, span in enumerate(spans)
    ]
    for copy in small + [c for pair in loads for c in pair]:
        copy.start()
    for copy in small:
        copy.wait()
    where_to = line[...]
    block = where_to // atoms
    slot = where_to - block * atoms
    extra = jnp.concatenate(
        [
            in_pieces(coords[...] * (1.0 / BOX)),
            block.astype(F32), slot.astype(F32), jnp.zeros((EXTRA - 11, atoms), F32),
        ],
        axis=0,
    ).astype(BF16)
    payload[atoms:] = extra
    side[0] = cot[...]

    def trig(span):
        return cos_sin_turns(mm(extra, thrice(lattice[:, span].astype(F32)), TN))

    acc = jnp.zeros((atoms, 2 * ch), F32)
    c, s = trig(spans[0])
    for j, span in enumerate(spans):
        for copy in loads[j]:
            copy.wait()
        f1 = kernels[1, span]
        f0 = kernels[0, span]
        cos_filt = jnp.concatenate([modes[1, span, :ch] * f1, modes[0, span, :ch] * f0], axis=1)
        sin_filt = jnp.concatenate([modes[1, span, ch:] * f1, modes[0, span, ch:] * f0], axis=1)
        acc = acc + mm(c, cos_filt) + mm(s, sin_filt)
        if j + 1 < steps:
            c, s = trig(spans[j + 1])
    slope = silu_slope(k_scale * acc)
    payload[:atoms] = (cot[...].astype(F32) * slope[:, :ch]).astype(BF16)
    slope0[...] = slope[:, ch:]
    side[1] = slope[:, ch:].astype(BF16)


def own_kernel(idx, lattice, modes, kernels, saved, filt, filters, lattice16):
    own, ch = filters.shape[1:]
    n_modes = lattice.shape[1]
    saved[...] = modes[...]
    filters[...] = kernels[...]
    for b in range(modes.shape[0]):
        f = kernels[b]
        filt[b, :own] = modes[b, :, :ch] * f
        filt[b, own:] = modes[b, :, ch:] * f
    rows = jnp.concatenate([lattice[...].astype(F32), jnp.zeros((5, n_modes), F32)], axis=0)
    rolled = pltpu.roll(rows, n_modes - idx[0] * own, 1)
    lattice16[...] = thrice(rolled[:3, :own])


def stack_kernel(*refs):
    *parts, out = refs
    at = 0
    for ref in parts:
        out[at : at + ref.shape[0]] = ref[...]
        at += ref.shape[0]


def trig_kernel(lattice16, *refs):
    *refs, tile = refs
    modes = lattice16.shape[1]
    n = lattice16[...]
    first = 0
    for ref in refs:
        count, rows, atoms = ref.shape
        pair = min(2, count)

        def one(p, _, ref=ref, first=first, rows=rows, atoms=atoms, pair=pair):
            x = jnp.concatenate(
                [ref[p * pair + j, rows - EXTRA :, :] for j in range(pair)], axis=1
            )
            c, s = cos_sin_turns(mm(n, x, TN))
            start = (first + p * pair) * atoms
            at = pl.ds(start if isinstance(p, int) else pl.multiple_of(start, atoms), pair * atoms)
            tile[:modes, at] = c
            tile[modes:, at] = s
            return 0

        if count == pair:
            one(0, 0)
        else:
            lax.fori_loop(0, count // pair, one, 0)
        first += count


def rows_of(refs, start, count):
    ch = refs[0].shape[2]
    return jnp.concatenate(
        [r[:, start : start + count, :].reshape(-1, ch) for r in refs], axis=0
    )


def joined(tiles):
    return jnp.concatenate([t[...] for t in tiles], axis=1)


def adjoint_kernel(tiles_n, *refs):
    tiles, blocks = refs[:tiles_n], refs[tiles_n:-2]
    keep, send = refs[-2:]
    part = mm(joined(tiles), rows_of(blocks, 0, blocks[0].shape[2]))
    keep[...] = part
    send[...] = part.astype(BF16)


def trig_adjoint_kernel(lattice16, tile, *refs):
    *blocks, new_tile, keep, send = refs
    trig_kernel(lattice16, *blocks[1:], new_tile)
    adjoint_kernel(2, tile, new_tile, *blocks, keep, send)


def filtered_adjoint(b, k_scale, ratio, core, part, got, saved, filters, fgrad, adj_ref):
    own, ch = filters.shape[1:]
    mine = fgrad.shape[0]
    adj = k_scale * (part[...] + got[...].astype(F32))
    adj_ref[...] = adj
    at = pl.ds(pl.multiple_of(core * mine, mine), mine)
    sin_at = pl.ds(pl.multiple_of(own + core * mine, mine), mine)
    fgrad[...] = adj_ref[at, :] * saved[b, at, :ch].astype(F32) + adj_ref[sin_at, :] * saved[
        b, at, ch:
    ].astype(F32)
    f = filters[b].astype(F32) * ratio
    return jnp.concatenate([adj[:own] * f, adj[own:] * f], axis=0).astype(BF16)


def pos_part(k_scale, tile, m, h, w, lattice16):
    own = lattice16.shape[1]
    weight = mm(w, jnp.concatenate([m, h], axis=1), NT)
    dtheta = tile[:own].astype(F32) * weight[own:] - tile[own:].astype(F32) * weight[:own]
    return (2.0 * math.pi / BOX * k_scale) * mm(lattice16[:8], dtheta.astype(BF16))


def block1_kernel(k_scale, ratio, core, tile_a, tile_b, *refs):
    part, got, saved, filters, fgrad, factor, keep, *sends, scr = refs
    fac = filtered_adjoint(1, k_scale, ratio, core[0], part, got, saved, filters, fgrad, scr)
    factor[...] = fac
    add = k_scale * mm(fac.T, joined((tile_a, tile_b)))
    at = 0
    atoms = keep.shape[2]
    for out in (keep, *sends):
        for p in range(out.shape[0]):
            out[p] = add[:, at : at + atoms].astype(out.dtype)
            at += atoms


def pos1_kernel(k_scale, n, tile_a, tile_b, *refs):
    blocks, h_blocks = refs[:n], refs[n : 2 * n]
    filt, factor, lattice16, pos = refs[2 * n :]
    atoms = blocks[0].shape[2]
    w = jnp.concatenate([filt[1], factor[...]], axis=1)
    m = rows_of(blocks, 0, atoms)
    h = rows_of(h_blocks, atoms, atoms)
    pos[...] = pos_part(k_scale, joined((tile_a, tile_b)), m, h, w, lattice16)


def block0_kernel(k_scale, ratio, n, core, tile_a, tile_b, *refs):
    blocks, h_blocks = refs[:n], refs[n : 2 * n]
    part, got, saved, filters, filt, lattice16, pos1, cot, fgrad, x, scr = refs[2 * n :]
    _, atoms, ch = blocks[0].shape
    tile = joined((tile_a, tile_b))
    fac = filtered_adjoint(0, k_scale, ratio, core[0], part, got, saved, filters, fgrad, scr)
    w = jnp.concatenate([filt[0], fac], axis=1)
    add = k_scale * mm(fac.T, tile)
    m = rows_of(blocks, 0, atoms)
    h = rows_of(h_blocks, 0, atoms)
    pos = pos1[...] + pos_part(k_scale, tile, m, h, w, lattice16)
    x[:ch] = add.astype(BF16)
    x[:ch, :atoms] = (add[:, :atoms] + cot[...]).astype(BF16)
    x[ch:] = jnp.concatenate([pos, jnp.zeros_like(pos)], axis=0).astype(BF16)


def target_rows(c_blocks, row):
    atoms = c_blocks[0].shape[2]
    return jnp.concatenate(
        [c[p, atoms + row : atoms + row + 1, :] for c in c_blocks for p in range(c.shape[0])],
        axis=1,
    ).astype(F32)


def hot_kernel(order, idx, *refs):
    *c_blocks, hot = refs
    atoms = c_blocks[0].shape[2]
    block = (target_rows(c_blocks, 9).astype(jnp.int32) ^ idx[0]).astype(F32)
    rows = jnp.concatenate(
        [block, target_rows(c_blocks, 10), jnp.zeros((6, block.shape[1]), F32)], axis=0
    )
    cols = rows.T
    shape = (block.shape[1], atoms)
    block = jnp.broadcast_to(cols[:, 0:1], shape).astype(BF16)
    slot = jnp.broadcast_to(cols[:, 1:2], shape).astype(BF16)
    lane = lax.broadcasted_iota(jnp.int32, shape, 1).astype(F32).astype(BF16)
    one = jnp.where(slot == lane, jnp.ones_like(lane), jnp.zeros_like(lane))
    for q, at in enumerate(order):
        here = block == jnp.full(shape, at, F32).astype(BF16)
        hot[:, q * atoms : (q + 1) * atoms] = jnp.where(here, one, jnp.zeros_like(one))


def place_kernel(first, x, hot, out):
    count, _, atoms = out.shape
    placed = mm(x[...], hot[:, first * atoms : (first + count) * atoms])
    for q in range(count):
        out[q] = placed[:, q * atoms : (q + 1) * atoms].astype(out.dtype)


def place_by_block_kernel(first, idx, order, x, *refs):
    *c_blocks, out, block, slot = refs
    count, _, atoms = out.shape
    block[...] = (target_rows(c_blocks, 9).astype(jnp.int32) ^ idx[0]).astype(F32)
    slot[...] = target_rows(c_blocks, 10)
    lanes = lax.broadcasted_iota(jnp.int32, (atoms, block.shape[1]), 0).astype(F32).astype(BF16)

    def one(q, _):
        target = order[first + q].astype(F32)
        here = jnp.where(block[...] == target, slot[...], -1.0).astype(BF16)
        hot = jnp.where(here == lanes, jnp.ones_like(lanes), jnp.zeros_like(lanes))
        out[q] = mm(x[...], hot, NT).astype(out.dtype)
        return 0

    lax.fori_loop(0, count, one, 0)


def reduce_kernel(got_n, both, keep, *refs):
    got = refs[:got_n]
    rest, *sends = refs[got_n:]
    width = rest.shape[0]
    for p in range(keep.shape[0]):
        total = functools.reduce(lambda a, g: a + g[p].astype(F32), got, keep[p])
        if p < width:
            rest[p] = total
        if both:
            sends[0][p] = total.astype(BF16)
        elif p >= width:
            sends[p // width - 1][p % width] = total.astype(BF16)


def finish1_kernel(keep, got, cot, slope0, far, cot_t, msg):
    own = cot[...].astype(F32).T + keep[0] + got[1].astype(F32)
    cot_t[...] = own
    msg[0] = (own.T * slope0[...]).astype(BF16)
    other = far[0].astype(F32).T + keep[1] + got[0].astype(F32)
    msg[1] = (other.T * far[1].astype(F32)).astype(BF16)


def finish0_kernel(keep, *refs):
    got = refs[:-2]
    feat, pos = refs[-2:]
    total = functools.reduce(lambda a, g: a + g[0].astype(F32), got, keep[0])
    ch = feat.shape[1]
    feat[...] = total[:ch].T
    pos[...] = total[ch : ch + 3]


def filters_kernel(f0, f1, out):
    out[0] = f0[...]
    out[1] = f1[...]


VMEM = pl.BlockSpec(memory_space=pltpu.VMEM)
PARAMS = pltpu.CompilerParams(vmem_limit_bytes=24 << 20)
SMEM = pl.BlockSpec(memory_space=pltpu.SMEM)
HBM = pl.BlockSpec(memory_space=pltpu.HBM)


def near(x):
    return pltpu.with_memory_space_constraint(x, pltpu.VMEM)


def far(x):
    return pltpu.with_memory_space_constraint(x, pltpu.HBM)


def call(kernel, outs, *args, scalars=0, scratch=(), alias=None):
    specs = [SMEM] * scalars + [VMEM] * (len(args) - scalars)
    args = args[:scalars] + tuple(near(a) for a in args[scalars:])
    return pl.pallas_call(
        kernel,
        out_shape=outs,
        in_specs=specs,
        out_specs=jax.tree.map(lambda _: VMEM, outs),
        scratch_shapes=list(scratch),
        input_output_aliases=alias or {},
        compiler_params=PARAMS,
    )(*args)


def buf(shape, dtype):
    return pltpu.VMEM(shape, dtype)


def sds(shape, dtype):
    return jax.ShapeDtypeStruct(shape, dtype)


def swap(x, mask, devices):
    return lax.ppermute(x, "atoms", [(i, i ^ mask) for i in range(devices)])


def phase_plan(devices):
    bits = devices.bit_length() - 1
    return [[1 << b] for b in range(bits - 1, 2, -1)] + [[2, 4, 6]]


def position_order(plan):
    order = [0]
    for masks in plan:
        order = order + [p ^ m for m in masks for p in order]
    return order


def stack(parts):
    count = sum(p.shape[0] for p in parts)
    return call(stack_kernel, buf((count, *parts[0].shape[1:]), parts[0].dtype), *parts)


def swaps(arrays, masks, devices):
    out = []
    for y, m in zip(arrays, masks):
        out.append(swap(y, m, devices))
    return out


def gather(y, plan, devices, start=0):
    for k in range(start, len(plan)):
        got = swaps([y] * len(plan[k]), plan[k], devices)
        if k < len(plan) - 1:
            y = stack([y, *got])
    return [y, *got]


def reduce_blocks(keep, got, plan, devices, both=False):
    for k in range(len(plan) - 1, -1, -1):
        masks = plan[k]
        if got:
            swap_all = both and k == 0
            width = keep.shape[0] if swap_all else keep.shape[0] // (len(masks) + 1)
            block = (width, *keep.shape[1:])
            keep, *sends = call(
                functools.partial(reduce_kernel, len(got), swap_all),
                (buf(block, F32),) + (buf(block, BF16),) * len(masks),
                keep, *got,
            )
        got = swaps(sends, masks, devices)
    return keep, got


def stages(coords, lattice, hidden, modes, kernels, cot, line):
    blocks = hidden.shape[0]
    channels = hidden.shape[2]
    n_modes = lattice.shape[1]
    atoms = coords.shape[1]
    devices = lax.axis_size("atoms")
    chips = devices // 2
    own = n_modes // chips
    mine = n_modes // devices
    side_atoms = atoms * chips
    k_scale = n_modes ** (-0.5)
    ratio = (atoms * devices) ** (-0.5) / k_scale
    plan = phase_plan(devices)
    order = position_order(plan)
    order = order + [p ^ 1 for p in order]
    me = lax.axis_index("atoms").reshape(1).astype(jnp.int32)
    chip = me // 2
    core = me % 2

    chunk = min(CHUNK, n_modes)
    rows = atoms + EXTRA
    atom_stage = pl.pallas_call(
        functools.partial(atom_kernel, k_scale, chunk),
        in_specs=[HBM] * 6,
        out_specs=[VMEM] * 3,
        out_shape=(
            buf((rows, channels), BF16),
            buf((atoms, channels), F32),
            buf((2, atoms, channels), BF16),
        ),
        scratch_shapes=[
            pltpu.VMEM((3, atoms), F32),
            pltpu.VMEM((1, atoms), jnp.int32),
            pltpu.VMEM((3, n_modes), jnp.int32),
            pltpu.VMEM((blocks, n_modes, 2 * channels), BF16),
            pltpu.VMEM((blocks, n_modes, channels), BF16),
            pltpu.VMEM((atoms, channels), BF16),
            pltpu.SemaphoreType.DMA((4 + 2 * (n_modes // chunk),)),
        ],
        compiler_params=PARAMS,
    )
    h_blocks = gather(hidden.reshape(1, blocks * atoms, channels), plan, devices)
    payload, slope0, side = atom_stage(
        *(far(x) for x in (coords, line[None], lattice, modes, kernels, cot))
    )
    far_side = swap(side, plan[0][0], devices)

    own_rows = pl.pallas_call(
        own_kernel,
        grid_spec=pltpu.PrefetchScalarGridSpec(
            num_scalar_prefetch=1,
            grid=(1,),
            in_specs=[
                pl.BlockSpec((3, n_modes), lambda k, i: (0, 0)),
                pl.BlockSpec((blocks, own, 2 * channels), lambda k, i: (0, i[0], 0)),
                pl.BlockSpec((blocks, own, channels), lambda k, i: (0, i[0], 0)),
            ],
            out_specs=[VMEM] * 4,
        ),
        out_shape=(
            buf((blocks, own, 2 * channels), BF16),
            buf((blocks, 2 * own, channels), BF16),
            buf((blocks, own, channels), BF16),
            buf((EXTRA, own), BF16),
        ),
        compiler_params=PARAMS,
    )
    saved, filt, filters, lattice16 = own_rows(chip, far(lattice), far(modes), far(kernels))
    c_blocks = gather(payload[None], plan, devices)
    n = len(c_blocks)

    adjoint_shapes = (buf((2 * own, channels), F32), buf((2 * own, channels), BF16))
    early_atoms = c_blocks[0].shape[0] * atoms
    tile_a = call(trig_kernel, buf((2 * own, early_atoms), BF16), lattice16, c_blocks[0])
    tile_b, part, send = call(
        trig_adjoint_kernel,
        (buf((2 * own, side_atoms - early_atoms), BF16), *adjoint_shapes),
        lattice16, tile_a, *c_blocks,
    )
    tiles = (tile_a, tile_b)
    got = swap(send, 1, devices)
    scr = pltpu.VMEM((2 * own, channels), F32)
    width = chips // n
    fgrad1, factor1, keep, *sends = call(
        functools.partial(block1_kernel, k_scale, ratio),
        (
            buf((mine, channels), F32),
            buf((2 * own, channels), BF16),
            buf((width, channels, atoms), F32),
        )
        + (buf((width, channels, atoms), BF16),) * (n - 1),
        core, *tiles, part, got, saved, filters,
        scalars=1,
        scratch=(scr,),
    )
    got = swaps(sends, plan[-1], devices)
    keep, got = reduce_blocks(keep, got, plan[:-1], devices, both=True)
    cot_t, msg0 = call(
        finish1_kernel,
        (buf((channels, atoms), F32), buf((2, atoms, channels), BF16)),
        keep, *got, cot, slope0, far_side,
    )

    pos1 = call(
        functools.partial(pos1_kernel, k_scale, n),
        buf((8, side_atoms), F32),
        *tiles, *c_blocks, *h_blocks, filt, factor1, lattice16,
    )
    m_blocks = gather(msg0, plan, devices, start=1)
    part, send = call(
        functools.partial(adjoint_kernel, len(tiles)), adjoint_shapes, *tiles, *m_blocks
    )
    got = swap(send, 1, devices)
    fgrad0, x = call(
        functools.partial(block0_kernel, k_scale, ratio, n),
        (buf((mine, channels), F32), buf((rows, side_atoms), BF16)),
        core, *tiles, *m_blocks, *h_blocks, part, got,
        saved, filters, filt, lattice16, pos1, cot_t,
        scalars=1,
        scratch=(scr,),
    )
    hot_shape = (side_atoms, devices * atoms)
    if math.prod(hot_shape) <= HOT_LIMIT:
        hot = call(
            functools.partial(hot_kernel, order), buf(hot_shape, BF16), me, *c_blocks, scalars=1
        )

        def place(first, dtype):
            out = buf((chips, rows, atoms), dtype)
            return call(functools.partial(place_kernel, first), out, x, hot)

    else:

        def place(first, dtype):
            return call(
                functools.partial(place_by_block_kernel, first),
                buf((chips, rows, atoms), dtype),
                me, jnp.asarray(order, jnp.int32), x, *c_blocks,
                scalars=2,
                scratch=(pltpu.VMEM((1, side_atoms), F32), pltpu.VMEM((1, side_atoms), F32)),
            )

    send = place(chips, BF16)
    got = [swap(send, 1, devices)]
    keep = place(0, F32)
    filter_grad = pl.pallas_call(
        filters_kernel,
        out_shape=sds((blocks, mine, channels), F32),
        in_specs=[VMEM, VMEM],
        compiler_params=PARAMS,
    )(near(fgrad0), near(fgrad1))
    keep, got = reduce_blocks(keep, got, plan, devices)
    feat_grad, pos_grad = pl.pallas_call(
        finish0_kernel,
        out_shape=(sds((atoms, channels), F32), sds((3, atoms), F32)),
        in_specs=[VMEM] * (1 + len(got)),
        compiler_params=PARAMS,
    )(near(keep), *(near(g) for g in got))
    return feat_grad, pos_grad, filter_grad


def solution(mesh):
    in_specs = (
        P(None, ("groups", "atoms")),
        P(),
        P(None, ("groups", "atoms"), None),
        P("groups", None, None),
        P(),
        P(("groups", "atoms"), None),
        P(("groups", "atoms")),
    )
    out_specs = (
        P(("groups", "atoms"), None),
        P(None, ("groups", "atoms")),
        P(None, ("groups", "atoms"), None),
    )
    return jax.shard_map(stages, mesh=mesh, in_specs=in_specs, out_specs=out_specs, check_vma=False)
```

```python
import functools
import math

import jax
import jax.numpy as jnp
from jax import lax
from jax.experimental import pallas as pl
from jax.experimental.pallas import tpu as pltpu
from jax.sharding import PartitionSpec as P

BOX = 72
F32 = jnp.float32
BF16 = jnp.bfloat16


SIN_TURN = (
    6.283182818519537, -41.341421395846474, 81.59618380218637, -76.58009981278215,
    41.205391752072295, -12.271257446632072,
)
COS_TURN = (
    0.9999992216454128, -19.73898252044836, 64.92872667203969, -85.27239717269248,
    58.794038140320986, -21.07677956285326,
)
ROUNDER = 12582912.0

NN = (((1,), (0,)), ((), ()))
NT = (((1,), (1,)), ((), ()))
TN = (((0,), (0,)), ((), ()))
CHUNK = 1024
HOT_LIMIT = 4 << 20
EXTRA = 16


def mm(a, b, dims=NN):
    return lax.dot_general(a, b, dims, preferred_element_type=F32)


def horner(coefs, u):
    acc = coefs[-1] * u + coefs[-2]
    for c in coefs[-3::-1]:
        acc = acc * u + c
    return acc


def cos_sin_turns(t):
    r = t - ((t + ROUNDER) - ROUNDER)
    u = r * r
    return horner(COS_TURN, u).astype(BF16), (r * horner(SIN_TURN, u)).astype(BF16)


def silu_slope(x):
    s = 1.0 / (1.0 + jnp.exp(-x))
    return s * (1.0 + x * (1.0 - s))


def in_pieces(x):
    hi = x.astype(BF16).astype(F32)
    mid = (x - hi).astype(BF16).astype(F32)
    low = (x - hi - mid).astype(BF16).astype(F32)
    return jnp.concatenate([hi, mid, low], axis=0)


def thrice(n):
    zero = jnp.zeros((EXTRA - 9, n.shape[1]), F32)
    return jnp.concatenate([n, n, n, zero], axis=0).astype(BF16)


def start_all(copies):
    for copy in copies:
        copy.start()


def wait_all(copies):
    for copy in copies:
        copy.wait()


def filtered(modes, kernels, at):
    ch = kernels.shape[1]
    f = kernels[at]
    return modes[at, :ch] * f, modes[at, ch:] * f


def atom_kernel(
    k_scale, chunk, block, coords_far, line_far, lattice_far, modes_far, kernels_far, cot_far,
    payload, waves, coords, line, lattice, modes, kernels, cot, sems,
):
    atoms, ch = cot.shape
    steps = lattice.shape[1] // chunk
    spans = [slice(j * chunk, (j + 1) * chunk) for j in range(steps)]
    small = [
        pltpu.make_async_copy(src, dst, sems.at[k])
        for k, (src, dst) in enumerate(
            ((coords_far, coords), (line_far, line), (lattice_far, lattice), (cot_far, cot))
        )
    ]
    loads = [
        [
            pltpu.make_async_copy(src.at[block, span], dst.at[span], sems.at[4 + 2 * j + k])
            for k, (src, dst) in enumerate(((modes_far, modes), (kernels_far, kernels)))
        ]
        for j, span in enumerate(spans)
    ]
    start_all(small + [c for pair in loads for c in pair])
    wait_all(small)
    where_to = line[...]
    out_block = where_to // atoms
    slot = where_to - out_block * atoms
    extra = jnp.concatenate(
        [
            in_pieces(coords[...] * (1.0 / BOX)),
            out_block.astype(F32), slot.astype(F32), jnp.zeros((EXTRA - 11, atoms), F32),
        ],
        axis=0,
    ).astype(BF16)
    payload[atoms:] = extra

    def trig(span):
        waves[0, :, span], waves[1, :, span] = cos_sin_turns(
            mm(extra, thrice(lattice[:, span].astype(F32)), TN)
        )

    acc = jnp.zeros((atoms, ch), F32)
    early = (steps + 1) // 2
    for span in spans[:early]:
        trig(span)
    wait_all([c for pair in loads for c in pair])
    for j, span in enumerate(spans):
        if j >= early:
            trig(span)
        cos_filt, sin_filt = filtered(modes, kernels, span)
        acc = acc + mm(waves[0, :, span], cos_filt) + mm(waves[1, :, span], sin_filt)
    payload[:atoms] = (cot[...].astype(F32) * silu_slope(k_scale * acc)).astype(BF16)


def own_kernel(
    k_scale, chunk, chip, waves, cot, lattice, modes_far, kernels_far,
    slope0, side, saved, filt, filters, lattice16, modes, kernels, sems,
):
    blocks, own, ch = filters.shape
    n_modes = lattice.shape[1]
    steps = n_modes // chunk
    spans = [slice(j * chunk, (j + 1) * chunk) for j in range(steps)]
    loads = [
        [
            pltpu.make_async_copy(src.at[0, span], dst.at[span], sems.at[2 * j + k])
            for k, (src, dst) in enumerate(((modes_far, modes), (kernels_far, kernels)))
        ]
        for j, span in enumerate(spans)
    ]
    mine = pl.ds(pl.multiple_of(chip[0] * own, own), own)
    own_loads = [
        pltpu.make_async_copy(src.at[b, mine], dst.at[b], sems.at[2 * steps + 2 * (b - 1) + k])
        for b in range(1, blocks)
        for k, (src, dst) in enumerate(((modes_far, saved), (kernels_far, filters)))
    ]
    start_all([c for pair in loads for c in pair] + own_loads)
    side[0] = cot[...]
    rows = jnp.concatenate([lattice[...].astype(F32), jnp.zeros((5, n_modes), F32)], axis=0)
    rolled = pltpu.roll(rows, n_modes - chip[0] * own, 1)
    lattice16[...] = thrice(rolled[:3, :own])
    acc = jnp.zeros(slope0.shape, F32)
    for j, span in enumerate(spans):
        wait_all(loads[j])
        cos_filt, sin_filt = filtered(modes, kernels, span)
        acc = acc + mm(waves[0, :, span], cos_filt) + mm(waves[1, :, span], sin_filt)
    slope = silu_slope(k_scale * acc)
    slope0[...] = slope
    side[1] = slope.astype(BF16)
    saved[0] = modes[mine, :]
    filters[0] = kernels[mine, :]
    wait_all(own_loads)
    for b in range(blocks):
        f = filters[b]
        filt[b, :own] = saved[b, :, :ch] * f
        filt[b, own:] = saved[b, :, ch:] * f


def stack_kernel(*refs):
    *parts, out = refs
    at = 0
    for ref in parts:
        out[at : at + ref.shape[0]] = ref[...]
        at += ref.shape[0]


def trig_kernel(lattice16, *refs):
    *refs, tile = refs
    modes = lattice16.shape[1]
    n = lattice16[...]
    first = 0
    for ref in refs:
        count, rows, atoms = ref.shape
        pair = min(2, count)

        def one(p, _, ref=ref, first=first, rows=rows, atoms=atoms, pair=pair):
            x = jnp.concatenate(
                [ref[p * pair + j, rows - EXTRA :, :] for j in range(pair)], axis=1
            )
            c, s = cos_sin_turns(mm(n, x, TN))
            start = (first + p * pair) * atoms
            at = pl.ds(start if isinstance(p, int) else pl.multiple_of(start, atoms), pair * atoms)
            tile[:modes, at] = c
            tile[modes:, at] = s
            return 0

        if count == pair:
            one(0, 0)
        else:
            lax.fori_loop(0, count // pair, one, 0)
        first += count


def rows_of(refs, start, count):
    ch = refs[0].shape[2]
    return jnp.concatenate(
        [r[:, start : start + count, :].reshape(-1, ch) for r in refs], axis=0
    )


def joined(tiles):
    return jnp.concatenate([t[...] for t in tiles], axis=1)


def adjoint_kernel(tiles_n, *refs):
    tiles, blocks = refs[:tiles_n], refs[tiles_n:-2]
    keep, send = refs[-2:]
    part = mm(joined(tiles), rows_of(blocks, 0, blocks[0].shape[2]))
    keep[...] = part
    send[...] = part.astype(BF16)


def trig_adjoint_kernel(lattice16, tile, *refs):
    *blocks, new_tile, keep, send = refs
    trig_kernel(lattice16, *blocks[1:], new_tile)
    adjoint_kernel(2, tile, new_tile, *blocks, keep, send)


def filtered_adjoint(b, k_scale, ratio, core, part, got, saved, filters, fgrad, adj_ref):
    own, ch = filters.shape[1:]
    mine = fgrad.shape[0]
    adj = k_scale * (part[...] + got[...].astype(F32))
    adj_ref[...] = adj
    at = pl.ds(pl.multiple_of(core * mine, mine), mine)
    sin_at = pl.ds(pl.multiple_of(own + core * mine, mine), mine)
    fgrad[...] = adj_ref[at, :] * saved[b, at, :ch].astype(F32) + adj_ref[sin_at, :] * saved[
        b, at, ch:
    ].astype(F32)
    f = filters[b].astype(F32) * ratio
    return jnp.concatenate([adj[:own] * f, adj[own:] * f], axis=0).astype(BF16)


def pos_part(k_scale, tile, m, h, w, lattice16):
    own = lattice16.shape[1]
    weight = mm(w, jnp.concatenate([m, h], axis=1), NT)
    dtheta = tile[:own].astype(F32) * weight[own:] - tile[own:].astype(F32) * weight[:own]
    return (2.0 * math.pi / BOX * k_scale) * mm(lattice16[:8], dtheta.astype(BF16))


def block1_kernel(k_scale, ratio, core, tile_a, tile_b, *refs):
    part, got, saved, filters, fgrad, factor, keep, *sends, scr = refs
    fac = filtered_adjoint(1, k_scale, ratio, core[0], part, got, saved, filters, fgrad, scr)
    factor[...] = fac
    add = k_scale * mm(fac.T, joined((tile_a, tile_b)))
    at = 0
    atoms = keep.shape[2]
    for out in (keep, *sends):
        for p in range(out.shape[0]):
            out[p] = add[:, at : at + atoms].astype(out.dtype)
            at += atoms


def pos1_kernel(k_scale, n, tile_a, tile_b, *refs):
    *blocks, filt, factor, lattice16, pos = refs
    blocks, h_blocks = blocks[:n], blocks[n:]
    atoms = blocks[0].shape[2]
    w = jnp.concatenate([filt[1], factor[...]], axis=1)
    m = rows_of(blocks, 0, atoms)
    h = rows_of(h_blocks, atoms, atoms)
    pos[...] = pos_part(k_scale, joined((tile_a, tile_b)), m, h, w, lattice16)


def block0_kernel(k_scale, ratio, n, core, tile_a, tile_b, *refs):
    *blocks, part, got, saved, filters, filt, lattice16, pos1, cot, fgrad, x, scr = refs
    blocks, h_blocks = blocks[:n], blocks[n:]
    _, atoms, ch = blocks[0].shape
    tile = joined((tile_a, tile_b))
    fac = filtered_adjoint(0, k_scale, ratio, core[0], part, got, saved, filters, fgrad, scr)
    w = jnp.concatenate([filt[0], fac], axis=1)
    add = k_scale * mm(fac.T, tile)
    m = rows_of(blocks, 0, atoms)
    h = rows_of(h_blocks, 0, atoms)
    pos = pos1[...] + pos_part(k_scale, tile, m, h, w, lattice16)
    x[:ch] = add.astype(BF16)
    x[:ch, :atoms] = (add[:, :atoms] + cot[...]).astype(BF16)
    x[ch:] = jnp.concatenate([pos, jnp.zeros_like(pos)], axis=0).astype(BF16)


def target_rows(c_blocks, row):
    atoms = c_blocks[0].shape[2]
    return jnp.concatenate(
        [c[p, atoms + row : atoms + row + 1, :] for c in c_blocks for p in range(c.shape[0])],
        axis=1,
    ).astype(F32)


def hot_kernel(order, idx, *refs):
    *c_blocks, hot = refs
    atoms = c_blocks[0].shape[2]
    block = (target_rows(c_blocks, 9).astype(jnp.int32) ^ idx[0]).astype(F32)
    rows = jnp.concatenate(
        [block, target_rows(c_blocks, 10), jnp.zeros((6, block.shape[1]), F32)], axis=0
    )
    cols = rows.T
    shape = (block.shape[1], atoms)
    block = jnp.broadcast_to(cols[:, 0:1], shape).astype(BF16)
    slot = jnp.broadcast_to(cols[:, 1:2], shape).astype(BF16)
    lane = lax.broadcasted_iota(jnp.int32, shape, 1).astype(F32).astype(BF16)
    one = jnp.where(slot == lane, jnp.ones_like(lane), jnp.zeros_like(lane))
    for q, at in enumerate(order):
        here = block == jnp.full(shape, at, F32).astype(BF16)
        hot[:, q * atoms : (q + 1) * atoms] = jnp.where(here, one, jnp.zeros_like(one))


def place_kernel(first, x, hot, out):
    count, _, atoms = out.shape
    placed = mm(x[...], hot[:, first * atoms : (first + count) * atoms])
    for q in range(count):
        out[q] = placed[:, q * atoms : (q + 1) * atoms].astype(out.dtype)


def place_by_block_kernel(first, idx, order, x, *refs):
    *c_blocks, out, block, slot = refs
    count, _, atoms = out.shape
    block[...] = (target_rows(c_blocks, 9).astype(jnp.int32) ^ idx[0]).astype(F32)
    slot[...] = target_rows(c_blocks, 10)
    lanes = lax.broadcasted_iota(jnp.int32, (atoms, block.shape[1]), 0).astype(F32).astype(BF16)

    def one(q, _):
        target = order[first + q].astype(F32)
        here = jnp.where(block[...] == target, slot[...], -1.0).astype(BF16)
        hot = jnp.where(here == lanes, jnp.ones_like(lanes), jnp.zeros_like(lanes))
        out[q] = mm(x[...], hot, NT).astype(out.dtype)
        return 0

    lax.fori_loop(0, count, one, 0)


def reduce_kernel(got_n, both, keep, *refs):
    got = refs[:got_n]
    rest, *sends = refs[got_n:]
    width = rest.shape[0]
    for p in range(keep.shape[0]):
        total = functools.reduce(lambda a, g: a + g[p].astype(F32), got, keep[p])
        if p < width:
            rest[p] = total
        if both:
            sends[0][p] = total.astype(BF16)
        elif p >= width:
            sends[p // width - 1][p % width] = total.astype(BF16)


def finish1_kernel(keep, got, cot, slope0, far, cot_t, msg):
    own = cot[...].astype(F32).T + keep[0] + got[1].astype(F32)
    cot_t[...] = own
    msg[0] = (own.T * slope0[...]).astype(BF16)
    other = far[0].astype(F32).T + keep[1] + got[0].astype(F32)
    msg[1] = (other.T * far[1].astype(F32)).astype(BF16)


def finish0_kernel(keep, *refs):
    got = refs[:-2]
    feat, pos = refs[-2:]
    total = functools.reduce(lambda a, g: a + g[0].astype(F32), got, keep[0])
    ch = feat.shape[1]
    feat[...] = total[:ch].T
    pos[...] = total[ch : ch + 3]


def filters_kernel(f0, f1, out):
    out[0] = f0[...]
    out[1] = f1[...]


VMEM = pl.BlockSpec(memory_space=pltpu.VMEM)
PARAMS = pltpu.CompilerParams(vmem_limit_bytes=24 << 20)
SMEM = pl.BlockSpec(memory_space=pltpu.SMEM)
HBM = pl.BlockSpec(memory_space=pltpu.HBM)


def near(x):
    return pltpu.with_memory_space_constraint(x, pltpu.VMEM)


def far(x):
    return pltpu.with_memory_space_constraint(x, pltpu.HBM)


def call(kernel, outs, *args, scalars=0, scratch=(), alias=None):
    specs = [SMEM] * scalars + [VMEM] * (len(args) - scalars)
    args = args[:scalars] + tuple(near(a) for a in args[scalars:])
    return pl.pallas_call(
        kernel,
        out_shape=outs,
        in_specs=specs,
        out_specs=jax.tree.map(lambda _: VMEM, outs),
        scratch_shapes=list(scratch),
        input_output_aliases=alias or {},
        compiler_params=PARAMS,
    )(*args)


def buf(shape, dtype):
    return pltpu.VMEM(shape, dtype)


def sds(shape, dtype):
    return jax.ShapeDtypeStruct(shape, dtype)


def swap(x, mask, devices):
    return lax.ppermute(x, "atoms", [(i, i ^ mask) for i in range(devices)])


def phase_plan(devices):
    bits = devices.bit_length() - 1
    return [[1 << b] for b in range(bits - 1, 2, -1)] + [[2, 4, 6]]


def position_order(plan):
    order = [0]
    for masks in plan:
        order = order + [p ^ m for m in masks for p in order]
    return order


def stack(parts):
    count = sum(p.shape[0] for p in parts)
    return call(stack_kernel, buf((count, *parts[0].shape[1:]), parts[0].dtype), *parts)


def swaps(arrays, masks, devices):
    out = []
    for y, m in zip(arrays, masks):
        out.append(swap(y, m, devices))
    return out


def gather(y, plan, devices, start=0):
    for k in range(start, len(plan)):
        got = swaps([y] * len(plan[k]), plan[k], devices)
        if k < len(plan) - 1:
            y = stack([y, *got])
    return [y, *got]


def reduce_blocks(keep, got, plan, devices, both=False):
    for k in range(len(plan) - 1, -1, -1):
        masks = plan[k]
        if got:
            swap_all = both and k == 0
            width = keep.shape[0] if swap_all else keep.shape[0] // (len(masks) + 1)
            block = (width, *keep.shape[1:])
            keep, *sends = call(
                functools.partial(reduce_kernel, len(got), swap_all),
                (buf(block, F32),) + (buf(block, BF16),) * len(masks),
                keep, *got,
            )
        got = swaps(sends, masks, devices)
    return keep, got


def stages(coords, lattice, hidden, modes, kernels, cot, line):
    blocks = hidden.shape[0]
    channels = hidden.shape[2]
    n_modes = lattice.shape[1]
    atoms = coords.shape[1]
    devices = lax.axis_size("atoms")
    chips = devices // 2
    own = n_modes // chips
    mine = n_modes // devices
    side_atoms = atoms * chips
    k_scale = n_modes ** (-0.5)
    ratio = (atoms * devices) ** (-0.5) / k_scale
    plan = phase_plan(devices)
    h_plan = plan[:-1] + [[2], [4]]
    order = position_order(plan)
    order = order + [p ^ 1 for p in order]
    me = lax.axis_index("atoms").reshape(1).astype(jnp.int32)
    chip = me // 2
    core = me % 2

    chunk = min(CHUNK, n_modes)
    rows = atoms + EXTRA
    steps = n_modes // chunk
    atom_stage = pl.pallas_call(
        functools.partial(atom_kernel, k_scale, chunk, blocks - 1),
        in_specs=[HBM] * 6,
        out_specs=[VMEM] * 2,
        out_shape=(buf((rows, channels), BF16), buf((2, atoms, n_modes), BF16)),
        scratch_shapes=[
            pltpu.VMEM((3, atoms), F32),
            pltpu.VMEM((1, atoms), jnp.int32),
            pltpu.VMEM((3, n_modes), jnp.int32),
            pltpu.VMEM((n_modes, 2 * channels), BF16),
            pltpu.VMEM((n_modes, channels), BF16),
            pltpu.VMEM((atoms, channels), BF16),
            pltpu.SemaphoreType.DMA((4 + 2 * steps,)),
        ],
        compiler_params=PARAMS,
    )
    h_blocks = gather(hidden.reshape(1, blocks * atoms, channels), h_plan, devices)
    payload, waves = atom_stage(
        *(far(x) for x in (coords, line[None], lattice, modes, kernels, cot))
    )
    own_stage = pl.pallas_call(
        functools.partial(own_kernel, k_scale, chunk),
        in_specs=[SMEM, VMEM, VMEM, VMEM, HBM, HBM],
        out_specs=[VMEM] * 6,
        out_shape=(
            buf((atoms, channels), F32),
            buf((2, atoms, channels), BF16),
            buf((blocks, own, 2 * channels), BF16),
            buf((blocks, 2 * own, channels), BF16),
            buf((blocks, own, channels), BF16),
            buf((EXTRA, own), BF16),
        ),
        scratch_shapes=[
            pltpu.VMEM((n_modes, 2 * channels), BF16),
            pltpu.VMEM((n_modes, channels), BF16),
            pltpu.SemaphoreType.DMA((2 * steps + 2 * (blocks - 1),)),
        ],
        compiler_params=PARAMS,
    )
    slope0, side, saved, filt, filters, lattice16 = own_stage(
        chip, near(waves), near(cot), near(lattice), far(modes), far(kernels)
    )
    far_side = swap(side, plan[0][0], devices)

    c_blocks = gather(payload[None], plan, devices)
    n = len(c_blocks)

    adjoint_shapes = (buf((2 * own, channels), F32), buf((2 * own, channels), BF16))
    early_atoms = c_blocks[0].shape[0] * atoms
    tile_a = call(trig_kernel, buf((2 * own, early_atoms), BF16), lattice16, c_blocks[0])
    tile_b, part, send = call(
        trig_adjoint_kernel,
        (buf((2 * own, side_atoms - early_atoms), BF16), *adjoint_shapes),
        lattice16, tile_a, *c_blocks,
    )
    tiles = (tile_a, tile_b)
    got = swap(send, 1, devices)
    scr = pltpu.VMEM((2 * own, channels), F32)
    width = chips // n
    fgrad1, factor1, keep, *sends = call(
        functools.partial(block1_kernel, k_scale, ratio),
        (
            buf((mine, channels), F32),
            buf((2 * own, channels), BF16),
            buf((width, channels, atoms), F32),
        )
        + (buf((width, channels, atoms), BF16),) * (n - 1),
        core, *tiles, part, got, saved, filters,
        scalars=1,
        scratch=(scr,),
    )
    got = swaps(sends, plan[-1], devices)
    keep, got = reduce_blocks(keep, got, plan[:-1], devices, both=True)
    cot_t, msg0 = call(
        finish1_kernel,
        (buf((channels, atoms), F32), buf((2, atoms, channels), BF16)),
        keep, *got, cot, slope0, far_side,
    )

    pos1 = call(
        functools.partial(pos1_kernel, k_scale, n),
        buf((8, side_atoms), F32),
        *tiles, *c_blocks, *h_blocks, filt, factor1, lattice16,
    )
    m_blocks = gather(msg0, plan, devices, start=1)
    part, send = call(
        functools.partial(adjoint_kernel, len(tiles)), adjoint_shapes, *tiles, *m_blocks
    )
    got = swap(send, 1, devices)
    fgrad0, x = call(
        functools.partial(block0_kernel, k_scale, ratio, n),
        (buf((mine, channels), F32), buf((rows, side_atoms), BF16)),
        core, *tiles, *m_blocks, *h_blocks, part, got,
        saved, filters, filt, lattice16, pos1, cot_t,
        scalars=1,
        scratch=(scr,),
    )
    hot_shape = (side_atoms, devices * atoms)
    if math.prod(hot_shape) <= HOT_LIMIT:
        hot = call(
            functools.partial(hot_kernel, order), buf(hot_shape, BF16), me, *c_blocks, scalars=1
        )

        def place(first, dtype):
            out = buf((chips, rows, atoms), dtype)
            return call(functools.partial(place_kernel, first), out, x, hot)

    else:

        def place(first, dtype):
            return call(
                functools.partial(place_by_block_kernel, first),
                buf((chips, rows, atoms), dtype),
                me, jnp.asarray(order, jnp.int32), x, *c_blocks,
                scalars=2,
                scratch=(pltpu.VMEM((1, side_atoms), F32), pltpu.VMEM((1, side_atoms), F32)),
            )

    send = place(chips, BF16)
    got = [swap(send, 1, devices)]
    keep = place(0, F32)
    filter_grad = pl.pallas_call(
        filters_kernel,
        out_shape=sds((blocks, mine, channels), F32),
        in_specs=[VMEM, VMEM],
        compiler_params=PARAMS,
    )(near(fgrad0), near(fgrad1))
    keep, got = reduce_blocks(keep, got, plan, devices)
    feat_grad, pos_grad = pl.pallas_call(
        finish0_kernel,
        out_shape=(sds((atoms, channels), F32), sds((3, atoms), F32)),
        in_specs=[VMEM] * (1 + len(got)),
        compiler_params=PARAMS,
    )(near(keep), *(near(g) for g in got))
    return feat_grad, pos_grad, filter_grad


def solution(mesh):
    in_specs = (
        P(None, ("groups", "atoms")),
        P(),
        P(None, ("groups", "atoms"), None),
        P("groups", None, None),
        P(),
        P(("groups", "atoms"), None),
        P(("groups", "atoms")),
    )
    out_specs = (
        P(("groups", "atoms"), None),
        P(None, ("groups", "atoms")),
        P(None, ("groups", "atoms"), None),
    )
    return jax.shard_map(stages, mesh=mesh, in_specs=in_specs, out_specs=out_specs, check_vma=False)
```
